512 devices in a mesh: items: 32 (over x, y), cents: 16 (over z, core).
Axes of the slice: x: 4, y: 8, z: 8, core: 2. Of those that a mesh axis runs over, the one named last changes fastest.
Arguments:
- embeddings: bfloat16 [61440, 1024], P('items')
- counts: int32 [32], P('items'), may hold values from 1152 to 1920, as said below
- centroids: bfloat16 [2048, 1024], P('cents')
Outputs:
- final_centroids: bfloat16 [2048, 1024], P('cents')
The draws below stay inside these ranges and needn't reach their ends.
Inputs may be any that keep to these rules, and one draw needn't show every extreme that they name: The counts of replicas 0 to i-1 sum to 1536 * i plus an offset of at most 192 in either direction, reached both ways in every draw; all counts sum to 49152. Rows of a buffer past its count carry no data.
All inputs are finite; a program needn't handle non-finite values.
Results may differ from the reference program's by a relative error of at most 0.0112.
Values may be sent and summed in bfloat16 or wider, within the bound.
No kernel may reach another device: no remote copies, remote signals or barrier semaphores. Data moves between devices by JAX's collectives and lax.ppermute only.
A program may use at most 64 MiB of HBM per device.

```python
import jax
import jax.numpy as jnp
from jax import lax

D = 1024
CENTROIDS = 2048
ROWS_DEV = 1536
ITERS = 2
SPILL = 192
IN_CAP = 1920
N_ITEMS = 32


def cluster_draw(key):
    base = jax.random.normal(jax.random.fold_in(key, 11), (CENTROIDS, D), jnp.float32)
    return base


def draw_centroids(key, part):
    return cluster_draw(key).astype(jnp.bfloat16)


def draw_embeddings(key, part):
    total_rows = IN_CAP * N_ITEMS
    return jax.random.normal(jax.random.fold_in(key, 25), (total_rows, D), jnp.float32).astype(jnp.bfloat16)


def draw_counts(key, part):
    spread = jax.random.randint(jax.random.fold_in(key, 31), (N_ITEMS,), -SPILL, SPILL + 1).astype(jnp.int32)
    anchor = jax.random.randint(jax.random.fold_in(key, 32), (), 1, N_ITEMS - 3)
    position = jnp.arange(N_ITEMS)
    spread = jnp.where(position == 0, SPILL, spread)
    spread = jnp.where(position == anchor, -SPILL, spread)
    spread = jnp.where(position == anchor + 1, SPILL, spread)
    spread = jnp.where(position == anchor + 2, -SPILL, spread)
    spread = jnp.where(position == N_ITEMS - 1, 0, spread)
    spread = spread.astype(jnp.int32)
    previous = jnp.concatenate([jnp.zeros((1,), jnp.int32), spread[:-1]])
    return (ROWS_DEV + spread - previous).astype(jnp.int32)


def setup_inputs(seed: int = 0) -> dict:
    splits = jax.random.split(jax.random.key(seed), 4)
    return {
        "embeddings": draw_embeddings(jax.random.fold_in(splits[3], 71), 0),
        "counts": draw_counts(jax.random.fold_in(splits[3], 71), 0),
        "centroids": draw_centroids(jax.random.fold_in(splits[3], 71), 0),
    }


prior_count = 2.0


def reference(embeddings, counts, centroids):
    blocks = embeddings.reshape(N_ITEMS, IN_CAP, D)
    slots = jnp.arange(IN_CAP, dtype=jnp.int32)
    valid = slots[None, :] < counts[:, None].astype(jnp.int32)
    scale = D ** -0.5
    current = centroids
    for step in range(ITERS):
        cent_f = current.astype(jnp.float32)
        norms = jnp.sum(cent_f * cent_f, axis=1)

        def one_block(carry, item):
            rows_here, mask_here = item
            dots = jnp.dot(rows_here, current.T, preferred_element_type=jnp.float32)
            score = (2.0 * dots - norms[None, :]) * scale
            top = jnp.max(score, axis=1, keepdims=True)
            expo = jnp.exp(score - top)
            resp = (expo / jnp.sum(expo, axis=1, keepdims=True)).astype(jnp.bfloat16)
            resp = jnp.where(mask_here[:, None], resp, jnp.zeros_like(resp))
            moment = jnp.dot(resp.T, rows_here, preferred_element_type=jnp.float32)
            mass = jnp.sum(resp.astype(jnp.float32), axis=0)
            return (carry[0] + moment, carry[1] + mass), None

        start = (jnp.zeros((CENTROIDS, D), jnp.float32), jnp.zeros((CENTROIDS,), jnp.float32))
        (moment, mass), unused = lax.scan(one_block, start, (blocks, valid))
        current = ((moment + prior_count * cent_f) / (mass[:, None] + prior_count)).astype(jnp.bfloat16)
    return current
```

```python
import jax
import jax.numpy as jnp
from jax import lax
from jax.sharding import PartitionSpec as P

D = 1024
ITERS = 2
prior_count = 2.0


def gather_all(part, axis):
    count = lax.axis_size(axis)
    return lax.all_to_all(jnp.broadcast_to(part[None], (count,) + part.shape), axis, 0, 0)


def body(embeddings, counts, centroids):
    rows = embeddings.shape[0]
    cents = centroids.shape[0]
    n_items = lax.axis_size("items")
    own = cents // n_items
    place = lax.axis_index("items")
    scale = D ** (-0.5)
    valid = jnp.arange(rows, dtype=jnp.int32) < counts[0]
    current = centroids
    for step in range(ITERS):
        cent_f = current.astype(jnp.float32)
        norms = jnp.sum(cent_f * cent_f, axis=1)
        dots = lax.dot_general(
            current, embeddings, (((1,), (1,)), ((), ())), preferred_element_type=jnp.float32
        )
        score = (2.0 * dots - norms[:, None]) * scale
        top = jnp.max(score, axis=0)
        logs = top + jnp.log(jnp.sum(jnp.exp(score - top[None]), axis=0))
        all_logs = gather_all(logs, "cents")
        high = jnp.max(all_logs, axis=0)
        total = high + jnp.log(jnp.sum(jnp.exp(all_logs - high[None]), axis=0))
        resp = jnp.where(valid[None], jnp.exp(score - total[None]), 0.0).astype(jnp.bfloat16)
        mass = jnp.sum(resp.astype(jnp.float32), axis=1)
        moment = lax.dot_general(
            resp, embeddings, (((1,), (0,)), ((), ())), preferred_element_type=jnp.float32
        )
        mass_high = mass.astype(jnp.bfloat16)
        mass_low = (mass - mass_high.astype(jnp.float32)).astype(jnp.bfloat16)
        lanes = lax.broadcasted_iota(jnp.int32, (cents, 128), 1)
        masses = jnp.where(lanes == 0, mass_high[:, None], mass_low[:, None])
        sent = jnp.concatenate([moment.astype(jnp.bfloat16), masses], axis=1)
        parts = lax.all_to_all(sent.reshape(n_items, own, D + 128), "items", 0, 0)
        sums = jnp.sum(parts.astype(jnp.float32), axis=0)
        own_mass = sums[:, D] + sums[:, D + 1]
        before = lax.dynamic_slice_in_dim(current, place * own, own, 0).astype(jnp.float32)
        fresh = (sums[:, :D] + prior_count * before) / (own_mass[:, None] + prior_count)
        current = gather_all(fresh.astype(jnp.bfloat16), "items").reshape(cents, D)
    return current


def solution(mesh):
    in_specs = (P("items", None), P("items"), P("cents", None))
    out_specs = P("cents", None)
    return jax.shard_map(body, mesh=mesh, in_specs=in_specs, out_specs=out_specs, check_vma=False)
```

```python
import jax
import jax.numpy as jnp
from jax import lax
from jax.experimental import pallas as pl
from jax.experimental.pallas import tpu as pltpu
from jax.sharding import PartitionSpec as P

D = 1024
ITERS = 2
CHUNK = 384
HALF = D // 2
LANES = 128
OWN = 8
WIDE = HALF + LANES
prior_count = 2.0
scale = D ** (-0.5)

f32, bf16 = jnp.float32, jnp.bfloat16
vmem = pl.BlockSpec(memory_space=pltpu.VMEM)
smem = pl.BlockSpec(memory_space=pltpu.SMEM)
hbm = pl.BlockSpec(memory_space=pltpu.HBM)


def norms_of(cents):
    wide = cents.astype(f32)
    return jnp.sum(wide * wide, axis=1, keepdims=True) * scale


def score_chunk(cents, norms, rows, start, score_ref, logs_ref):
    size = rows.shape[0]
    dots = lax.dot_general(cents, rows, (((1,), (1,)), ((), ())), preferred_element_type=f32)
    score = dots * (2.0 * scale) - norms
    score_ref[:, pl.ds(start, size)] = score
    top = jnp.max(score, axis=0, keepdims=True)
    logs = top + jnp.log(jnp.sum(jnp.exp(score - top), axis=0, keepdims=True))
    for peer in range(logs_ref.shape[0]):
        logs_ref[peer, :, pl.ds(start, size)] = logs


def first_scores(count_ref, place_ref, rows_hbm, cents_ref, rows_ref, score_ref, logs_ref, known_ref, sems):
    known_ref[0] = count_ref[0]
    known_ref[1] = place_ref[0]
    total = rows_ref.shape[0]
    copies = [
        pltpu.make_async_copy(
            rows_hbm.at[pl.ds(start, CHUNK)], rows_ref.at[pl.ds(start, CHUNK)], sems.at[i]
        )
        for i, start in enumerate(range(0, total, CHUNK))
    ]
    for copy in copies:
        copy.start()
    cents = cents_ref[...]
    norms = norms_of(cents)
    for i, start in enumerate(range(0, total, CHUNK)):
        copies[i].wait()
        score_chunk(cents, norms, rows_ref[pl.ds(start, CHUNK), :], start, score_ref, logs_ref)


def later_scores(rows_ref, blocks_ref, score_ref, logs_ref):
    total = rows_ref.shape[0]
    n_cents = blocks_ref.shape[0] // 2
    cents = jnp.concatenate([blocks_ref[:n_cents, :], blocks_ref[n_cents:, :]], axis=1)
    norms = norms_of(cents)
    for start in range(0, total, CHUNK):
        score_chunk(cents, norms, rows_ref[pl.ds(start, CHUNK), :], start, score_ref, logs_ref)


def moments(known_ref, logs_ref, score_ref, rows_ref, out_ref):
    peers, _, total = logs_ref.shape
    n_cents = score_ref.shape[0]
    high = logs_ref[0]
    for peer in range(1, peers):
        high = jnp.maximum(high, logs_ref[peer])
    mass_all = jnp.exp(logs_ref[0] - high)
    for peer in range(1, peers):
        mass_all = mass_all + jnp.exp(logs_ref[peer] - high)
    logs = high + jnp.log(mass_all)
    valid = lax.broadcasted_iota(jnp.int32, (1, total), 1) < known_ref[0]
    resp = jnp.where(valid, jnp.exp(score_ref[...] - logs), 0.0).astype(bf16)
    mass = jnp.sum(resp.astype(f32), axis=1, keepdims=True)
    moment = jnp.dot(resp, rows_ref[...], preferred_element_type=f32)
    mass_high = mass.astype(bf16)
    mass_low = (mass - mass_high.astype(f32)).astype(bf16)
    lanes = lax.broadcasted_iota(jnp.int32, (n_cents, LANES), 1)
    masses = jnp.where(lanes == 0, mass_high.astype(f32), mass_low.astype(f32)).astype(bf16)
    for half in range(2):
        out_ref[pl.ds(half * n_cents, n_cents), :HALF] = moment[
            :, half * HALF : (half + 1) * HALF
        ].astype(bf16)
        out_ref[pl.ds(half * n_cents, n_cents), HALF:] = masses


def update(parts_ref, before, out_ref):
    own = before.shape[0]
    sums = parts_ref[:own, :].astype(f32)
    for part in range(1, parts_ref.shape[0] // own):
        sums = sums + parts_ref[pl.ds(part * own, own), :].astype(f32)
    mass = sums[:, HALF : HALF + 1] + sums[:, HALF + 1 : HALF + 2]
    fresh = (sums[:, :HALF] + prior_count * before) / (mass + prior_count)
    fresh = fresh.astype(bf16)
    for part in range(out_ref.shape[0] // own):
        out_ref[pl.ds(part * own, own), :] = fresh


def first_update(known_ref, parts_ref, cents_ref, out_ref):
    n_cents = cents_ref.shape[0]
    own = OWN
    per_half = n_cents // own
    place = known_ref[1]
    row = pl.multiple_of(lax.rem(place, per_half) * own, own)
    mine = cents_ref[pl.ds(row, own), :].astype(f32)
    before = jnp.where(place < per_half, mine[:, :HALF], mine[:, HALF:])
    update(parts_ref, before, out_ref)


def later_update(parts_ref, fresh_ref, out_ref):
    update(parts_ref, fresh_ref[:OWN, :].astype(f32), out_ref)


def join(blocks_ref, out_ref):
    n_cents = out_ref.shape[0]
    for half in range(2):
        out_ref[:, half * HALF : (half + 1) * HALF] = blocks_ref[pl.ds(half * n_cents, n_cents), :]


def params(mib):
    return pltpu.CompilerParams(vmem_limit_bytes=mib << 20)


def body(embeddings, counts, centroids):
    total, n_cents = embeddings.shape[0], centroids.shape[0]
    n_items, n_split = lax.axis_size("items"), lax.axis_size("cents")
    place = lax.axis_index("items").astype(jnp.int32)[None]
    score_shape = pltpu.VMEM((n_cents, total), f32)
    logs_shape = pltpu.VMEM((n_split, 1, total), f32)
    sent_shape = pltpu.VMEM((2 * n_cents, WIDE), bf16)
    block_shape = pltpu.VMEM((2 * n_cents, HALF), bf16)

    def exchange(x, axis):
        count = lax.axis_size(axis)
        split = x.reshape(count, x.shape[0] // count, *x.shape[1:])
        return lax.all_to_all(split, axis, 0, 0).reshape(x.shape)

    rows, score, logs, known = pl.pallas_call(
        first_scores,
        out_shape=(pltpu.VMEM(embeddings.shape, bf16), score_shape, logs_shape, pltpu.SMEM((2,), jnp.int32)),
        in_specs=[smem, smem, hbm, vmem],
        out_specs=(vmem, vmem, vmem, smem),
        scratch_shapes=[pltpu.SemaphoreType.DMA((total // CHUNK,))],
        compiler_params=params(57),
        name="first_scores",
    )(counts, place, embeddings, centroids)
    fresh = blocks = None
    for step in range(ITERS):
        if step:
            score, logs = pl.pallas_call(
                later_scores,
                out_shape=(score_shape, logs_shape),
                in_specs=[vmem, vmem],
                out_specs=(vmem, vmem),
                compiler_params=params(16),
                name="later_scores",
            )(rows, blocks)
        logs = lax.all_to_all(logs, "cents", 0, 0)
        sent = pl.pallas_call(
            moments,
            out_shape=sent_shape,
            in_specs=[smem, vmem, vmem, vmem],
            out_specs=vmem,
            compiler_params=params(16),
            name="moments",
        )(known, logs, score, rows)
        parts = exchange(sent, "items")
        if step:
            fresh = pl.pallas_call(
                later_update,
                out_shape=block_shape,
                in_specs=[vmem, vmem],
                out_specs=vmem,
                compiler_params=params(16),
                name="later_update",
            )(parts, fresh)
        else:
            fresh = pl.pallas_call(
                first_update,
                out_shape=block_shape,
                in_specs=[smem, vmem, vmem],
                out_specs=vmem,
                compiler_params=params(16),
                name="first_update",
            )(known, parts, centroids)
        blocks = exchange(fresh, "items")
    return pl.pallas_call(
        join,
        out_shape=jax.ShapeDtypeStruct(centroids.shape, bf16),
        in_specs=[vmem],
        out_specs=vmem,
        compiler_params=params(16),
        name="join",
    )(blocks)


def solution(mesh):
    in_specs = (P("items", None), P("items"), P("cents", None))
    out_specs = P("cents", None)
    return jax.shard_map(body, mesh=mesh, in_specs=in_specs, out_specs=out_specs, check_vma=False)
```

```python
import jax
import jax.numpy as jnp
from jax import lax
from jax.experimental import pallas as pl
from jax.experimental.pallas import tpu as pltpu
from jax.sharding import PartitionSpec as P

D = 1024
ITERS = 2
CHUNK = 384
LANES = 128
TILE = 8
WIDE = D + LANES
prior_count = 2.0
scale = D ** (-0.5)

f32, bf16 = jnp.float32, jnp.bfloat16
vmem = pl.BlockSpec(memory_space=pltpu.VMEM)
smem = pl.BlockSpec(memory_space=pltpu.SMEM)
hbm = pl.BlockSpec(memory_space=pltpu.HBM)


def norms_of(cents):
    wide = cents.astype(f32)
    return jnp.sum(wide * wide, axis=1, keepdims=True) * scale


def score_chunk(cents, norms, rows, start, score_ref, logs_ref):
    size = rows.shape[0]
    dots = lax.dot_general(cents, rows, (((1,), (1,)), ((), ())), preferred_element_type=f32)
    score = dots * (2.0 * scale) - norms
    score_ref[:, pl.ds(start, size)] = score
    top = jnp.max(score, axis=0, keepdims=True)
    logs = top + jnp.log(jnp.sum(jnp.exp(score - top), axis=0, keepdims=True))
    for peer in range(logs_ref.shape[0]):
        logs_ref[peer, :, pl.ds(start, size)] = logs


def first_scores(
    count_ref, place_ref, rows_hbm, cents_hbm, rows_ref, score_ref, logs_ref, known_ref, cents_ref, sems
):
    total = rows_ref.shape[0]
    starts = range(0, total, CHUNK)
    cents_copy = pltpu.make_async_copy(cents_hbm, cents_ref, sems.at[len(starts)])
    cents_copy.start()
    copies = [
        pltpu.make_async_copy(
            rows_hbm.at[pl.ds(start, CHUNK)], rows_ref.at[pl.ds(start, CHUNK)], sems.at[i]
        )
        for i, start in enumerate(starts)
    ]
    for copy in copies:
        copy.start()
    known_ref[0] = count_ref[0]
    known_ref[1] = place_ref[0]
    cents_copy.wait()
    cents = cents_ref[...]
    norms = norms_of(cents)
    for copy, start in zip(copies, starts):
        copy.wait()
        score_chunk(cents, norms, rows_ref[pl.ds(start, CHUNK), :], start, score_ref, logs_ref)


def flat(blocks_ref):
    parts, own, width = blocks_ref.shape
    return blocks_ref[...].reshape(parts * own, width)


def later_scores(rows_ref, blocks_ref, score_ref, logs_ref):
    total = rows_ref.shape[0]
    cents = flat(blocks_ref)
    norms = norms_of(cents)
    for start in range(0, total, CHUNK):
        score_chunk(cents, norms, rows_ref[pl.ds(start, CHUNK), :], start, score_ref, logs_ref)


def moments(known_ref, logs_ref, score_ref, rows_ref, out_ref):
    peers, _, total = logs_ref.shape
    n_cents = score_ref.shape[0]
    high = logs_ref[0]
    for peer in range(1, peers):
        high = jnp.maximum(high, logs_ref[peer])
    mass_all = jnp.exp(logs_ref[0] - high)
    for peer in range(1, peers):
        mass_all = mass_all + jnp.exp(logs_ref[peer] - high)
    logs = high + jnp.log(mass_all)
    valid = lax.broadcasted_iota(jnp.int32, (1, total), 1) < known_ref[0]
    resp = jnp.where(valid, jnp.exp(score_ref[...] - logs), 0.0).astype(bf16)
    mass = jnp.sum(resp.astype(f32), axis=1, keepdims=True)
    moment = jnp.dot(resp, rows_ref[...], preferred_element_type=f32)
    mass_high = mass.astype(bf16)
    mass_low = (mass - mass_high.astype(f32)).astype(bf16)
    lanes = lax.broadcasted_iota(jnp.int32, (n_cents, LANES), 1)
    masses = jnp.where(lanes == 0, mass_high.astype(f32), mass_low.astype(f32)).astype(bf16)
    parts, own, _ = out_ref.shape
    out_ref[:, :, :D] = moment.astype(bf16).reshape(parts, own, D)
    out_ref[:, :, D:] = masses.reshape(parts, own, LANES)


def update(parts_ref, before, out_ref):
    sums = parts_ref[0].astype(f32)
    for part in range(1, parts_ref.shape[0]):
        sums = sums + parts_ref[part].astype(f32)
    mass = sums[:, D : D + 1] + sums[:, D + 1 : D + 2]
    fresh = ((sums[:, :D] + prior_count * before) / (mass + prior_count)).astype(bf16)
    for part in range(out_ref.shape[0]):
        out_ref[part] = fresh


def first_update(known_ref, parts_ref, cents_ref, out_ref):
    own = out_ref.shape[1]
    place = known_ref[1]
    row = pl.multiple_of(place * own // TILE * TILE, TILE)
    near = cents_ref[pl.ds(row, TILE), :].astype(f32)
    before = near[:own]
    for skip in range(own, TILE, own):
        before = jnp.where(place * own == row + skip, near[skip : skip + own], before)
    update(parts_ref, before, out_ref)


def later_update(parts_ref, fresh_ref, out_ref):
    update(parts_ref, fresh_ref[0].astype(f32), out_ref)


def join(blocks_ref, out_ref):
    out_ref[...] = flat(blocks_ref)


def params(mib):
    return pltpu.CompilerParams(vmem_limit_bytes=mib << 20)


def body(embeddings, counts, centroids):
    total, n_cents = embeddings.shape[0], centroids.shape[0]
    n_items, n_split = lax.axis_size("items"), lax.axis_size("cents")
    place = lax.axis_index("items").astype(jnp.int32)[None]
    score_shape = pltpu.VMEM((n_cents, total), f32)
    logs_shape = pltpu.VMEM((n_split, 1, total), f32)
    sent_shape = pltpu.VMEM((n_items, n_cents // n_items, WIDE), bf16)
    block_shape = pltpu.VMEM((n_items, n_cents // n_items, D), bf16)

    rows, score, logs, known = pl.pallas_call(
        first_scores,
        out_shape=(pltpu.VMEM(embeddings.shape, bf16), score_shape, logs_shape, pltpu.SMEM((2,), jnp.int32)),
        in_specs=[smem, smem, hbm, hbm],
        out_specs=(vmem, vmem, vmem, smem),
        scratch_shapes=[
            pltpu.VMEM(centroids.shape, bf16),
            pltpu.SemaphoreType.DMA((total // CHUNK + 1,)),
        ],
        compiler_params=params(57),
        name="first_scores",
    )(counts, place, embeddings, centroids)
    fresh = blocks = None
    for step in range(ITERS):
        if step:
            score, logs = pl.pallas_call(
                later_scores,
                out_shape=(score_shape, logs_shape),
                in_specs=[vmem, vmem],
                out_specs=(vmem, vmem),
                compiler_params=params(16),
                name="later_scores",
            )(rows, blocks)
        logs = lax.all_to_all(logs, "cents", 0, 0)
        sent = pl.pallas_call(
            moments,
            out_shape=sent_shape,
            in_specs=[smem, vmem, vmem, vmem],
            out_specs=vmem,
            compiler_params=params(16),
            name="moments",
        )(known, logs, score, rows)
        parts = lax.all_to_all(sent, "items", 0, 0)
        if step:
            fresh = pl.pallas_call(
                later_update,
                out_shape=block_shape,
                in_specs=[vmem, vmem],
                out_specs=vmem,
                compiler_params=params(16),
                name="later_update",
            )(parts, fresh)
        else:
            fresh = pl.pallas_call(
                first_update,
                out_shape=block_shape,
                in_specs=[smem, vmem, vmem],
                out_specs=vmem,
                compiler_params=params(16),
                name="first_update",
            )(known, parts, centroids)
        blocks = lax.all_to_all(fresh, "items", 0, 0)
    return pl.pallas_call(
        join,
        out_shape=jax.ShapeDtypeStruct(centroids.shape, bf16),
        in_specs=[vmem],
        out_specs=vmem,
        compiler_params=params(16),
        name="join",
    )(blocks)


def solution(mesh):
    in_specs = (P("items", None), P("items"), P("cents", None))
    out_specs = P("cents", None)
    return jax.shard_map(body, mesh=mesh, in_specs=in_specs, out_specs=out_specs, check_vma=False)
```

```python
import jax
import jax.numpy as jnp
from jax import lax
from jax.experimental import pallas as pl
from jax.experimental.pallas import tpu as pltpu
from jax.sharding import PartitionSpec as P

D = 1024
ITERS = 2
CHUNK = 128
PIECE = 384
EARLY = 2
LANES = 128
TILE = 8
WIDE = D + LANES
prior_count = 2.0
scale = D ** (-0.5)

f32, bf16 = jnp.float32, jnp.bfloat16
vmem = pl.BlockSpec(memory_space=pltpu.VMEM)
smem = pl.BlockSpec(memory_space=pltpu.SMEM)
hbm = pl.BlockSpec(memory_space=pltpu.HBM)


def norms_of(cents):
    wide = cents.astype(f32)
    return jnp.sum(wide * wide, axis=1, keepdims=True) * scale


def dot_chunk(cents, norms, rows_ref, start, size, score_ref):
    rows = rows_ref[pl.ds(start, size), :]
    dots = lax.dot_general(cents, rows, (((1,), (1,)), ((), ())), preferred_element_type=f32)
    score_ref[:, pl.ds(start, size)] = dots * (2.0 * scale) - norms


def logs_chunk(score_ref, start, size, logs_ref):
    score = score_ref[:, pl.ds(start, size)]
    top = jnp.max(score, axis=0, keepdims=True)
    logs = top + jnp.log(jnp.sum(jnp.exp(score - top), axis=0, keepdims=True))
    for peer in range(logs_ref.shape[0]):
        logs_ref[peer, :, pl.ds(start, size)] = logs


def score_span(cents, norms, rows_ref, first, last, score_ref, logs_ref):
    for start in range(first, last, CHUNK):
        dot_chunk(cents, norms, rows_ref, start, CHUNK, score_ref)
        logs_chunk(score_ref, start, CHUNK, logs_ref)


def first_scores(
    count_ref, place_ref, rows_hbm, cents_hbm, rows_ref, score_ref, logs_ref, known_ref, cents_ref, sems
):
    total = rows_ref.shape[0]
    starts = range(0, total, PIECE)
    cents_copy = pltpu.make_async_copy(cents_hbm, cents_ref, sems.at[len(starts)])
    cents_copy.start()
    copies = [
        pltpu.make_async_copy(
            rows_hbm.at[pl.ds(start, PIECE)], rows_ref.at[pl.ds(start, PIECE)], sems.at[i]
        )
        for i, start in enumerate(starts)
    ]
    for copy in copies:
        copy.start()
    known_ref[0] = count_ref[0]
    known_ref[1] = place_ref[0]
    cents_copy.wait()
    cents = cents_ref[...]
    norms = norms_of(cents)
    for copy in copies[:EARLY]:
        copy.wait()
    score_span(cents, norms, rows_ref, 0, EARLY * PIECE, score_ref, logs_ref)
    for copy in copies[EARLY:]:
        copy.wait()
    score_span(cents, norms, rows_ref, EARLY * PIECE, total, score_ref, logs_ref)


def flat(blocks_ref):
    parts, own, width = blocks_ref.shape
    return blocks_ref[...].reshape(parts * own, width)


def later_scores(rows_ref, blocks_ref, score_ref, logs_ref):
    cents = flat(blocks_ref)
    score_span(cents, norms_of(cents), rows_ref, 0, rows_ref.shape[0], score_ref, logs_ref)


def moments(known_ref, logs_ref, score_ref, rows_ref, out_ref):
    peers, _, total = logs_ref.shape
    n_cents = score_ref.shape[0]
    high = logs_ref[0]
    for peer in range(1, peers):
        high = jnp.maximum(high, logs_ref[peer])
    mass_all = jnp.exp(logs_ref[0] - high)
    for peer in range(1, peers):
        mass_all = mass_all + jnp.exp(logs_ref[peer] - high)
    logs = high + jnp.log(mass_all)
    valid = lax.broadcasted_iota(jnp.int32, (1, total), 1) < known_ref[0]
    resp = jnp.where(valid, jnp.exp(score_ref[...] - logs), 0.0).astype(bf16)
    mass = jnp.sum(resp.astype(f32), axis=1, keepdims=True)
    moment = jnp.dot(resp, rows_ref[...], preferred_element_type=f32)
    mass_high = mass.astype(bf16)
    mass_low = (mass - mass_high.astype(f32)).astype(bf16)
    lanes = lax.broadcasted_iota(jnp.int32, (n_cents, LANES), 1)
    masses = jnp.where(lanes == 0, mass_high.astype(f32), mass_low.astype(f32)).astype(bf16)
    parts, own, _ = out_ref.shape
    out_ref[:, :, :D] = moment.astype(bf16).reshape(parts, own, D)
    out_ref[:, :, D:] = masses.reshape(parts, own, LANES)


def update(parts_ref, before, out_ref):
    sums = parts_ref[0].astype(f32)
    for part in range(1, parts_ref.shape[0]):
        sums = sums + parts_ref[part].astype(f32)
    mass = sums[:, D : D + 1] + sums[:, D + 1 : D + 2]
    fresh = ((sums[:, :D] + prior_count * before) / (mass + prior_count)).astype(bf16)
    for part in range(out_ref.shape[0]):
        out_ref[part] = fresh


def first_update(known_ref, parts_ref, cents_ref, out_ref):
    own = out_ref.shape[1]
    place = known_ref[1]
    row = pl.multiple_of(place * own // TILE * TILE, TILE)
    near = cents_ref[pl.ds(row, TILE), :].astype(f32)
    before = near[:own]
    for skip in range(own, TILE, own):
        before = jnp.where(place * own == row + skip, near[skip : skip + own], before)
    update(parts_ref, before, out_ref)


def later_update(parts_ref, fresh_ref, out_ref):
    update(parts_ref, fresh_ref[0].astype(f32), out_ref)


def join(blocks_ref, out_ref):
    out_ref[...] = flat(blocks_ref)


def params(mib):
    return pltpu.CompilerParams(vmem_limit_bytes=mib << 20)


def body(embeddings, counts, centroids):
    total, n_cents = embeddings.shape[0], centroids.shape[0]
    n_items, n_split = lax.axis_size("items"), lax.axis_size("cents")
    place = lax.axis_index("items").astype(jnp.int32)[None]
    score_shape = pltpu.VMEM((n_cents, total), f32)
    logs_shape = pltpu.VMEM((n_split, 1, total), f32)
    sent_shape = pltpu.VMEM((n_items, n_cents // n_items, WIDE), bf16)
    block_shape = pltpu.VMEM((n_items, n_cents // n_items, D), bf16)

    rows, score, logs, known = pl.pallas_call(
        first_scores,
        out_shape=(pltpu.VMEM(embeddings.shape, bf16), score_shape, logs_shape, pltpu.SMEM((2,), jnp.int32)),
        in_specs=[smem, smem, hbm, hbm],
        out_specs=(vmem, vmem, vmem, smem),
        scratch_shapes=[
            pltpu.VMEM(centroids.shape, bf16),
            pltpu.SemaphoreType.DMA((total // PIECE + 1,)),
        ],
        compiler_params=params(57),
        name="first_scores",
    )(counts, place, embeddings, centroids)
    fresh = blocks = None
    for step in range(ITERS):
        if step:
            score, logs = pl.pallas_call(
                later_scores,
                out_shape=(score_shape, logs_shape),
                in_specs=[vmem, vmem],
                out_specs=(vmem, vmem),
                compiler_params=params(16),
                name="later_scores",
            )(rows, blocks)
        logs = lax.all_to_all(logs, "cents", 0, 0)
        sent = pl.pallas_call(
            moments,
            out_shape=sent_shape,
            in_specs=[smem, vmem, vmem, vmem],
            out_specs=vmem,
            compiler_params=params(16),
            name="moments",
        )(known, logs, score, rows)
        parts = lax.all_to_all(sent, "items", 0, 0)
        if step:
            fresh = pl.pallas_call(
                later_update,
                out_shape=block_shape,
                in_specs=[vmem, vmem],
                out_specs=vmem,
                compiler_params=params(16),
                name="later_update",
            )(parts, fresh)
        else:
            fresh = pl.pallas_call(
                first_update,
                out_shape=block_shape,
                in_specs=[smem, vmem, vmem],
                out_specs=vmem,
                compiler_params=params(16),
                name="first_update",
            )(known, parts, centroids)
        blocks = lax.all_to_all(fresh, "items", 0, 0)
    return pl.pallas_call(
        join,
        out_shape=jax.ShapeDtypeStruct(centroids.shape, bf16),
        in_specs=[vmem],
        out_specs=vmem,
        compiler_params=params(16),
        name="join",
    )(blocks)


def solution(mesh):
    in_specs = (P("items", None), P("items"), P("cents", None))
    out_specs = P("cents", None)
    return jax.shard_map(body, mesh=mesh, in_specs=in_specs, out_specs=out_specs, check_vma=False)
```

```python
import jax
import jax.numpy as jnp
from jax import lax
from jax.experimental import pallas as pl
from jax.experimental.pallas import tpu as pltpu
from jax.sharding import PartitionSpec as P

D = 1024
ITERS = 2
CHUNK = 128
PIECE = 384
EARLY = 2
LANES = 128
TILE = 8
HALF = D // 2
SUB = 4
prior_count = 2.0
scale = D ** (-0.5)

f32, bf16 = jnp.float32, jnp.bfloat16
vmem = pl.BlockSpec(memory_space=pltpu.VMEM)
smem = pl.BlockSpec(memory_space=pltpu.SMEM)
hbm = pl.BlockSpec(memory_space=pltpu.HBM)


def norms_of(cents):
    wide = cents.astype(f32)
    return jnp.sum(wide * wide, axis=1, keepdims=True) * scale


def dot_chunk(cents, norms, rows_ref, start, size, score_ref):
    rows = rows_ref[pl.ds(start, size), :]
    dots = lax.dot_general(cents, rows, (((1,), (1,)), ((), ())), preferred_element_type=f32)
    score_ref[:, pl.ds(start, size)] = dots * (2.0 * scale) - norms


def logs_chunk(score_ref, start, size, logs_ref):
    score = score_ref[:, pl.ds(start, size)]
    top = jnp.max(score, axis=0, keepdims=True)
    logs = top + jnp.log(jnp.sum(jnp.exp(score - top), axis=0, keepdims=True))
    for peer in range(logs_ref.shape[0]):
        logs_ref[peer, :, pl.ds(start, size)] = logs


def score_span(cents, norms, rows_ref, first, last, score_ref, logs_ref):
    for start in range(first, last, CHUNK):
        dot_chunk(cents, norms, rows_ref, start, CHUNK, score_ref)
        logs_chunk(score_ref, start, CHUNK, logs_ref)


def first_scores(
    count_ref, place_ref, rows_hbm, cents_hbm, rows_ref, score_ref, logs_ref, known_ref, cents_ref, sems
):
    total = rows_ref.shape[0]
    starts = range(0, total, PIECE)
    cents_copy = pltpu.make_async_copy(cents_hbm, cents_ref, sems.at[len(starts)])
    cents_copy.start()
    copies = [
        pltpu.make_async_copy(
            rows_hbm.at[pl.ds(start, PIECE)], rows_ref.at[pl.ds(start, PIECE)], sems.at[i]
        )
        for i, start in enumerate(starts)
    ]
    for copy in copies:
        copy.start()
    known_ref[0] = count_ref[0]
    known_ref[1] = place_ref[0]
    cents_copy.wait()
    cents = cents_ref[...]
    norms = norms_of(cents)
    for copy in copies[:EARLY]:
        copy.wait()
    score_span(cents, norms, rows_ref, 0, EARLY * PIECE, score_ref, logs_ref)
    for copy in copies[EARLY:]:
        copy.wait()
    score_span(cents, norms, rows_ref, EARLY * PIECE, total, score_ref, logs_ref)


def later_scores(rows_ref, cents_ref, score_ref, logs_ref):
    cents = cents_ref[...]
    score_span(cents, norms_of(cents), rows_ref, 0, rows_ref.shape[0], score_ref, logs_ref)


def moments(known_ref, logs_ref, score_ref, rows_ref, out_ref):
    peers, _, total = logs_ref.shape
    n_cents = score_ref.shape[0]
    high = logs_ref[0]
    for peer in range(1, peers):
        high = jnp.maximum(high, logs_ref[peer])
    mass_all = jnp.exp(logs_ref[0] - high)
    for peer in range(1, peers):
        mass_all = mass_all + jnp.exp(logs_ref[peer] - high)
    logs = high + jnp.log(mass_all)
    valid = lax.broadcasted_iota(jnp.int32, (1, total), 1) < known_ref[0]
    resp = jnp.where(valid, jnp.exp(score_ref[...] - logs), 0.0).astype(bf16)
    mass = jnp.sum(resp.astype(f32), axis=1, keepdims=True)
    moment = jnp.dot(resp, rows_ref[...], preferred_element_type=f32)
    groups, halves = out_ref.shape[:2]
    pieces = HALF // LANES
    for half in range(halves):
        for piece in range(pieces):
            start = half * HALF + piece * LANES
            tile = moment[:, start : start + LANES].astype(bf16).reshape(groups, 2, SUB, LANES)
            for low in range(2):
                out_ref[:, half, low * pieces + piece] = tile[:, low]
    mass_high = mass.astype(bf16).astype(f32)
    lanes = lax.broadcasted_iota(jnp.int32, (n_cents, LANES), 1)
    masses = jnp.where(lanes % 2 == 0, mass_high, mass - mass_high).reshape(groups, 2, SUB, LANES)
    lanes = lax.broadcasted_iota(jnp.int32, (groups, SUB, LANES), 2)
    tile = jnp.where(lanes < 2, masses[:, 0], masses[:, 1]).astype(bf16)
    for half in range(halves):
        out_ref[:, half, 2 * pieces] = tile


def update(parts_ref, before, out_ref):
    sums = parts_ref[0].astype(f32)
    for part in range(1, parts_ref.shape[0]):
        sums = sums + parts_ref[part].astype(f32)
    pieces = HALF // LANES
    masses = sums[2 * pieces]
    rows = []
    for low in range(2):
        mass = masses[:, 2 * low : 2 * low + 1] + masses[:, 2 * low + 1 : 2 * low + 2]
        moment = jnp.concatenate([sums[low * pieces + piece] for piece in range(pieces)], axis=1)
        old = before[low * SUB : (low + 1) * SUB]
        rows.append((moment + prior_count * old) / (mass + prior_count))
    fresh = jnp.concatenate(rows, axis=0).astype(bf16)
    for part in range(out_ref.shape[0]):
        out_ref[part] = fresh


def first_update(known_ref, parts_ref, cents_ref, out_ref):
    place = known_ref[1]
    row = pl.multiple_of(place // 2 * TILE, TILE)
    near = cents_ref[pl.ds(row, TILE), :].astype(f32)
    update(parts_ref, jnp.where(place % 2 == 0, near[:, :HALF], near[:, HALF:]), out_ref)


def later_update(parts_ref, fresh_ref, out_ref):
    update(parts_ref, fresh_ref[0].astype(f32), out_ref)


def params(mib):
    return pltpu.CompilerParams(vmem_limit_bytes=mib << 20)


def body(embeddings, counts, centroids):
    total, n_cents = embeddings.shape[0], centroids.shape[0]
    n_items, n_split = lax.axis_size("items"), lax.axis_size("cents")
    place = lax.axis_index("items").astype(jnp.int32)[None]
    score_shape = pltpu.VMEM((n_cents, total), f32)
    logs_shape = pltpu.VMEM((n_split, 1, total), f32)
    sent_shape = pltpu.VMEM((n_cents // TILE, 2, 2 * HALF // LANES + 1, SUB, LANES), bf16)
    block_shape = pltpu.VMEM((n_items, TILE, HALF), bf16)

    rows, score, logs, known = pl.pallas_call(
        first_scores,
        out_shape=(pltpu.VMEM(embeddings.shape, bf16), score_shape, logs_shape, pltpu.SMEM((2,), jnp.int32)),
        in_specs=[smem, smem, hbm, hbm],
        out_specs=(vmem, vmem, vmem, smem),
        scratch_shapes=[
            pltpu.VMEM(centroids.shape, bf16),
            pltpu.SemaphoreType.DMA((total // PIECE + 1,)),
        ],
        compiler_params=params(57),
        name="first_scores",
    )(counts, place, embeddings, centroids)
    fresh = current = None
    for step in range(ITERS):
        if step:
            score, logs = pl.pallas_call(
                later_scores,
                out_shape=(score_shape, logs_shape),
                in_specs=[vmem, vmem],
                out_specs=(vmem, vmem),
                compiler_params=params(16),
                name="later_scores",
            )(rows, current)
        logs = lax.all_to_all(logs, "cents", 0, 0)
        sent = pl.pallas_call(
            moments,
            out_shape=sent_shape,
            in_specs=[smem, vmem, vmem, vmem],
            out_specs=vmem,
            compiler_params=params(16),
            name="moments",
        )(known, logs, score, rows)
        parts = lax.all_to_all(sent.reshape(n_items, *sent.shape[2:]), "items", 0, 0)
        if step:
            fresh = pl.pallas_call(
                later_update,
                out_shape=block_shape,
                in_specs=[vmem, vmem],
                out_specs=vmem,
                compiler_params=params(16),
                name="later_update",
            )(parts, fresh)
        else:
            fresh = pl.pallas_call(
                first_update,
                out_shape=block_shape,
                in_specs=[smem, vmem, vmem],
                out_specs=vmem,
                compiler_params=params(16),
                name="first_update",
            )(known, parts, centroids)
        blocks = lax.all_to_all(fresh, "items", 0, 0)
        blocks = blocks.reshape(n_cents // TILE, 2, TILE, HALF).transpose(0, 2, 1, 3)
        current = blocks.reshape(n_cents, D)
    return current


def solution(mesh):
    in_specs = (P("items", None), P("items"), P("cents", None))
    out_specs = P("cents", None)
    return jax.shard_map(body, mesh=mesh, in_specs=in_specs, out_specs=out_specs, check_vma=False)
```

```python
import jax
import jax.numpy as jnp
from jax import lax
from jax.experimental import pallas as pl
from jax.experimental.pallas import tpu as pltpu
from jax.sharding import PartitionSpec as P

D = 1024
ITERS = 2
CHUNK = 128
PIECE = 384
EARLY = 2
LANES = 128
TILE = 8
HALF = D // 2
SUB = 4
prior_count = 2.0
X, Y = 4, 8
ORDER = [[x * Y + y for y in range(Y) for x in range(X)]]
scale = D ** (-0.5)

f32, bf16 = jnp.float32, jnp.bfloat16
vmem = pl.BlockSpec(memory_space=pltpu.VMEM)
smem = pl.BlockSpec(memory_space=pltpu.SMEM)
hbm = pl.BlockSpec(memory_space=pltpu.HBM)


def norms_of(cents):
    wide = cents.astype(f32)
    return jnp.sum(wide * wide, axis=1, keepdims=True) * scale


def dot_chunk(cents, norms, rows_ref, start, size, score_ref):
    rows = rows_ref[pl.ds(start, size), :]
    dots = lax.dot_general(cents, rows, (((1,), (1,)), ((), ())), preferred_element_type=f32)
    score_ref[:, pl.ds(start, size)] = dots * (2.0 * scale) - norms


def logs_chunk(score_ref, start, size, logs_ref):
    score = score_ref[:, pl.ds(start, size)]
    top = jnp.max(score, axis=0, keepdims=True)
    logs = top + jnp.log(jnp.sum(jnp.exp(score - top), axis=0, keepdims=True))
    for peer in range(logs_ref.shape[0]):
        logs_ref[peer, :, pl.ds(start, size)] = logs


def score_span(cents, norms, rows_ref, first, last, score_ref, logs_ref):
    for start in range(first, last, CHUNK):
        dot_chunk(cents, norms, rows_ref, start, CHUNK, score_ref)
        logs_chunk(score_ref, start, CHUNK, logs_ref)


def first_scores(
    count_ref, place_ref, rows_hbm, cents_hbm, rows_ref, score_ref, logs_ref, known_ref, cents_ref, sems
):
    total = rows_ref.shape[0]
    starts = range(0, total, PIECE)
    cents_copy = pltpu.make_async_copy(cents_hbm, cents_ref, sems.at[len(starts)])
    cents_copy.start()
    copies = [
        pltpu.make_async_copy(
            rows_hbm.at[pl.ds(start, PIECE)], rows_ref.at[pl.ds(start, PIECE)], sems.at[i]
        )
        for i, start in enumerate(starts)
    ]
    for copy in copies:
        copy.start()
    known_ref[0] = count_ref[0]
    known_ref[1] = place_ref[0]
    cents_copy.wait()
    cents = cents_ref[...]
    norms = norms_of(cents)
    for copy in copies[:EARLY]:
        copy.wait()
    score_span(cents, norms, rows_ref, 0, EARLY * PIECE, score_ref, logs_ref)
    for copy in copies[EARLY:]:
        copy.wait()
    score_span(cents, norms, rows_ref, EARLY * PIECE, total, score_ref, logs_ref)


def later_scores(rows_ref, cents_ref, score_ref, logs_ref):
    cents = cents_ref[...]
    score_span(cents, norms_of(cents), rows_ref, 0, rows_ref.shape[0], score_ref, logs_ref)


def moments(known_ref, logs_ref, score_ref, rows_ref, out_ref):
    peers, _, total = logs_ref.shape
    n_cents = score_ref.shape[0]
    high = logs_ref[0]
    for peer in range(1, peers):
        high = jnp.maximum(high, logs_ref[peer])
    mass_all = jnp.exp(logs_ref[0] - high)
    for peer in range(1, peers):
        mass_all = mass_all + jnp.exp(logs_ref[peer] - high)
    logs = high + jnp.log(mass_all)
    valid = lax.broadcasted_iota(jnp.int32, (1, total), 1) < known_ref[0]
    resp = jnp.where(valid, jnp.exp(score_ref[...] - logs), 0.0).astype(bf16)
    mass = jnp.sum(resp.astype(f32), axis=1, keepdims=True)
    moment = jnp.dot(resp, rows_ref[...], preferred_element_type=f32)
    groups, halves = out_ref.shape[:2]
    pieces = HALF // LANES
    for half in range(halves):
        for piece in range(pieces):
            start = half * HALF + piece * LANES
            tile = moment[:, start : start + LANES].astype(bf16).reshape(groups, 2, SUB, LANES)
            for low in range(2):
                out_ref[:, half, low * pieces + piece] = tile[:, low]
    mass_high = mass.astype(bf16).astype(f32)
    lanes = lax.broadcasted_iota(jnp.int32, (n_cents, LANES), 1)
    masses = jnp.where(lanes % 2 == 0, mass_high, mass - mass_high).reshape(groups, 2, SUB, LANES)
    lanes = lax.broadcasted_iota(jnp.int32, (groups, SUB, LANES), 2)
    tile = jnp.where(lanes < 2, masses[:, 0], masses[:, 1]).astype(bf16)
    for half in range(halves):
        out_ref[:, half, 2 * pieces] = tile


def update(parts_ref, before, out_ref):
    sums = parts_ref[0].astype(f32)
    for part in range(1, parts_ref.shape[0]):
        sums = sums + parts_ref[part].astype(f32)
    pieces = HALF // LANES
    masses = sums[2 * pieces]
    rows = []
    for low in range(2):
        mass = masses[:, 2 * low : 2 * low + 1] + masses[:, 2 * low + 1 : 2 * low + 2]
        moment = jnp.concatenate([sums[low * pieces + piece] for piece in range(pieces)], axis=1)
        old = before[low * SUB : (low + 1) * SUB]
        rows.append((moment + prior_count * old) / (mass + prior_count))
    fresh = jnp.concatenate(rows, axis=0).astype(bf16)
    for part in range(out_ref.shape[0]):
        out_ref[part] = fresh


def first_update(known_ref, parts_ref, cents_ref, out_ref):
    place = known_ref[1]
    row = pl.multiple_of(place // 2 * TILE, TILE)
    near = cents_ref[pl.ds(row, TILE), :].astype(f32)
    update(parts_ref, jnp.where(place % 2 == 0, near[:, :HALF], near[:, HALF:]), out_ref)


def later_update(parts_ref, fresh_ref, out_ref):
    update(parts_ref, fresh_ref[0].astype(f32), out_ref)


def params(mib):
    return pltpu.CompilerParams(vmem_limit_bytes=mib << 20)


def body(embeddings, counts, centroids):
    total, n_cents = embeddings.shape[0], centroids.shape[0]
    n_items, n_split = lax.axis_size("items"), lax.axis_size("cents")
    item = lax.axis_index("items").astype(jnp.int32)
    place = (item % Y * X + item // Y)[None]
    score_shape = pltpu.VMEM((n_cents, total), f32)
    logs_shape = pltpu.VMEM((n_split, 1, total), f32)
    sent_shape = pltpu.VMEM((n_cents // TILE, 2, 2 * HALF // LANES + 1, SUB, LANES), bf16)
    block_shape = pltpu.VMEM((n_items, TILE, HALF), bf16)

    rows, score, logs, known = pl.pallas_call(
        first_scores,
        out_shape=(pltpu.VMEM(embeddings.shape, bf16), score_shape, logs_shape, pltpu.SMEM((2,), jnp.int32)),
        in_specs=[smem, smem, hbm, hbm],
        out_specs=(vmem, vmem, vmem, smem),
        scratch_shapes=[
            pltpu.VMEM(centroids.shape, bf16),
            pltpu.SemaphoreType.DMA((total // PIECE + 1,)),
        ],
        compiler_params=params(57),
        name="first_scores",
    )(counts, place, embeddings, centroids)
    fresh = current = None
    for step in range(ITERS):
        if step:
            score, logs = pl.pallas_call(
                later_scores,
                out_shape=(score_shape, logs_shape),
                in_specs=[vmem, vmem],
                out_specs=(vmem, vmem),
                compiler_params=params(16),
                name="later_scores",
            )(rows, current)
        logs = lax.all_to_all(logs, "cents", 0, 0)
        sent = pl.pallas_call(
            moments,
            out_shape=sent_shape,
            in_specs=[smem, vmem, vmem, vmem],
            out_specs=vmem,
            compiler_params=params(16),
            name="moments",
        )(known, logs, score, rows)
        parts = lax.all_to_all(sent.reshape(n_items, *sent.shape[2:]), "items", 0, 0, axis_index_groups=ORDER)
        if step:
            fresh = pl.pallas_call(
                later_update,
                out_shape=block_shape,
                in_specs=[vmem, vmem],
                out_specs=vmem,
                compiler_params=params(16),
                name="later_update",
            )(parts, fresh)
        else:
            fresh = pl.pallas_call(
                first_update,
                out_shape=block_shape,
                in_specs=[smem, vmem, vmem],
                out_specs=vmem,
                compiler_params=params(16),
                name="first_update",
            )(known, parts, centroids)
        blocks = lax.all_to_all(fresh, "items", 0, 0, axis_index_groups=ORDER)
        blocks = blocks.reshape(n_cents // TILE, 2, TILE, HALF).transpose(0, 2, 1, 3)
        current = blocks.reshape(n_cents, D)
    return current


def solution(mesh):
    in_specs = (P("items", None), P("items"), P("cents", None))
    out_specs = P("cents", None)
    return jax.shard_map(body, mesh=mesh, in_specs=in_specs, out_specs=out_specs, check_vma=False)
```

```python
import jax
import jax.numpy as jnp
from jax import lax
from jax.experimental import pallas as pl
from jax.experimental.pallas import tpu as pltpu
from jax.sharding import PartitionSpec as P

D = 1024
ITERS = 2
CHUNK = 128
PIECE = 384
EARLY = 2
LANES = 128
TILE = 8
HALF = D // 2
SUB = 4
prior_count = 2.0
X, Y = 4, 8
ORDER = [[x * Y + y for y in range(Y) for x in range(X)]]
Z, CORE = 8, 2
CENT_ORDER = [[z * CORE + core for core in range(CORE) for z in range(Z)]]
scale = D ** (-0.5)

f32, bf16 = jnp.float32, jnp.bfloat16
vmem = pl.BlockSpec(memory_space=pltpu.VMEM)
smem = pl.BlockSpec(memory_space=pltpu.SMEM)
hbm = pl.BlockSpec(memory_space=pltpu.HBM)


def norms_of(cents):
    wide = cents.astype(f32)
    return jnp.sum(wide * wide, axis=1, keepdims=True) * scale


def dot_chunk(cents, norms, rows_ref, start, size, score_ref):
    rows = rows_ref[pl.ds(start, size), :]
    dots = lax.dot_general(cents, rows, (((1,), (1,)), ((), ())), preferred_element_type=f32)
    score_ref[:, pl.ds(start, size)] = dots * (2.0 * scale) - norms


def logs_chunk(score_ref, start, size, logs_ref):
    score = score_ref[:, pl.ds(start, size)]
    top = jnp.max(score, axis=0, keepdims=True)
    logs = top + jnp.log(jnp.sum(jnp.exp(score - top), axis=0, keepdims=True))
    for peer in range(logs_ref.shape[0]):
        logs_ref[peer, :, pl.ds(start, size)] = logs


def score_span(cents, norms, rows_ref, first, last, score_ref, logs_ref):
    for start in range(first, last, CHUNK):
        dot_chunk(cents, norms, rows_ref, start, CHUNK, score_ref)
        logs_chunk(score_ref, start, CHUNK, logs_ref)


def first_scores(
    count_ref, place_ref, rows_hbm, cents_hbm, rows_ref, score_ref, logs_ref, known_ref, cents_ref, sems
):
    total = rows_ref.shape[0]
    starts = range(0, total, PIECE)
    cents_copy = pltpu.make_async_copy(cents_hbm, cents_ref, sems.at[len(starts)])
    cents_copy.start()
    copies = [
        pltpu.make_async_copy(
            rows_hbm.at[pl.ds(start, PIECE)], rows_ref.at[pl.ds(start, PIECE)], sems.at[i]
        )
        for i, start in enumerate(starts)
    ]
    for copy in copies:
        copy.start()
    known_ref[0] = count_ref[0]
    known_ref[1] = place_ref[0]
    cents_copy.wait()
    cents = cents_ref[...]
    norms = norms_of(cents)
    for copy in copies[:EARLY]:
        copy.wait()
    score_span(cents, norms, rows_ref, 0, EARLY * PIECE, score_ref, logs_ref)
    for copy in copies[EARLY:]:
        copy.wait()
    score_span(cents, norms, rows_ref, EARLY * PIECE, total, score_ref, logs_ref)


def later_scores(rows_ref, cents_ref, score_ref, logs_ref):
    cents = cents_ref[...]
    score_span(cents, norms_of(cents), rows_ref, 0, rows_ref.shape[0], score_ref, logs_ref)


def moments(known_ref, logs_ref, score_ref, rows_ref, out_ref):
    peers, _, total = logs_ref.shape
    n_cents = score_ref.shape[0]
    high = logs_ref[0]
    for peer in range(1, peers):
        high = jnp.maximum(high, logs_ref[peer])
    mass_all = jnp.exp(logs_ref[0] - high)
    for peer in range(1, peers):
        mass_all = mass_all + jnp.exp(logs_ref[peer] - high)
    logs = high + jnp.log(mass_all)
    valid = lax.broadcasted_iota(jnp.int32, (1, total), 1) < known_ref[0]
    resp = jnp.where(valid, jnp.exp(score_ref[...] - logs), 0.0).astype(bf16)
    mass = jnp.sum(resp.astype(f32), axis=1, keepdims=True)
    moment = jnp.dot(resp, rows_ref[...], preferred_element_type=f32)
    groups, halves = out_ref.shape[:2]
    pieces = HALF // LANES
    for half in range(halves):
        for piece in range(pieces):
            start = half * HALF + piece * LANES
            tile = moment[:, start : start + LANES].astype(bf16).reshape(groups, 2, SUB, LANES)
            for low in range(2):
                out_ref[:, half, low * pieces + piece] = tile[:, low]
    mass_high = mass.astype(bf16).astype(f32)
    lanes = lax.broadcasted_iota(jnp.int32, (n_cents, LANES), 1)
    masses = jnp.where(lanes % 2 == 0, mass_high, mass - mass_high).reshape(groups, 2, SUB, LANES)
    lanes = lax.broadcasted_iota(jnp.int32, (groups, SUB, LANES), 2)
    tile = jnp.where(lanes < 2, masses[:, 0], masses[:, 1]).astype(bf16)
    for half in range(halves):
        out_ref[:, half, 2 * pieces] = tile


def update(parts_ref, before, out_ref):
    sums = parts_ref[0].astype(f32)
    for part in range(1, parts_ref.shape[0]):
        sums = sums + parts_ref[part].astype(f32)
    pieces = HALF // LANES
    masses = sums[2 * pieces]
    rows = []
    for low in range(2):
        mass = masses[:, 2 * low : 2 * low + 1] + masses[:, 2 * low + 1 : 2 * low + 2]
        moment = jnp.concatenate([sums[low * pieces + piece] for piece in range(pieces)], axis=1)
        old = before[low * SUB : (low + 1) * SUB]
        rows.append((moment + prior_count * old) / (mass + prior_count))
    fresh = jnp.concatenate(rows, axis=0).astype(bf16)
    for part in range(out_ref.shape[0]):
        out_ref[part] = fresh


def first_update(known_ref, parts_ref, cents_ref, out_ref):
    place = known_ref[1]
    row = pl.multiple_of(place // 2 * TILE, TILE)
    near = cents_ref[pl.ds(row, TILE), :].astype(f32)
    update(parts_ref, jnp.where(place % 2 == 0, near[:, :HALF], near[:, HALF:]), out_ref)


def later_update(parts_ref, fresh_ref, out_ref):
    update(parts_ref, fresh_ref[0].astype(f32), out_ref)


def params(mib):
    return pltpu.CompilerParams(vmem_limit_bytes=mib << 20)


def body(embeddings, counts, centroids):
    total, n_cents = embeddings.shape[0], centroids.shape[0]
    n_items, n_split = lax.axis_size("items"), lax.axis_size("cents")
    item = lax.axis_index("items").astype(jnp.int32)
    place = (item % Y * X + item // Y)[None]
    score_shape = pltpu.VMEM((n_cents, total), f32)
    logs_shape = pltpu.VMEM((n_split, 1, total), f32)
    sent_shape = pltpu.VMEM((n_cents // TILE, 2, 2 * HALF // LANES + 1, SUB, LANES), bf16)
    block_shape = pltpu.VMEM((n_items, TILE, HALF), bf16)

    rows, score, logs, known = pl.pallas_call(
        first_scores,
        out_shape=(pltpu.VMEM(embeddings.shape, bf16), score_shape, logs_shape, pltpu.SMEM((2,), jnp.int32)),
        in_specs=[smem, smem, hbm, hbm],
        out_specs=(vmem, vmem, vmem, smem),
        scratch_shapes=[
            pltpu.VMEM(centroids.shape, bf16),
            pltpu.SemaphoreType.DMA((total // PIECE + 1,)),
        ],
        compiler_params=params(57),
        name="first_scores",
    )(counts, place, embeddings, centroids)
    fresh = current = None
    for step in range(ITERS):
        if step:
            score, logs = pl.pallas_call(
                later_scores,
                out_shape=(score_shape, logs_shape),
                in_specs=[vmem, vmem],
                out_specs=(vmem, vmem),
                compiler_params=params(16),
                name="later_scores",
            )(rows, current)
        logs = lax.all_to_all(logs, "cents", 0, 0, axis_index_groups=CENT_ORDER)
        sent = pl.pallas_call(
            moments,
            out_shape=sent_shape,
            in_specs=[smem, vmem, vmem, vmem],
            out_specs=vmem,
            compiler_params=params(16),
            name="moments",
        )(known, logs, score, rows)
        parts = lax.all_to_all(sent.reshape(n_items, *sent.shape[2:]), "items", 0, 0, axis_index_groups=ORDER)
        if step:
            fresh = pl.pallas_call(
                later_update,
                out_shape=block_shape,
                in_specs=[vmem, vmem],
                out_specs=vmem,
                compiler_params=params(16),
                name="later_update",
            )(parts, fresh)
        else:
            fresh = pl.pallas_call(
                first_update,
                out_shape=block_shape,
                in_specs=[smem, vmem, vmem],
                out_specs=vmem,
                compiler_params=params(16),
                name="first_update",
            )(known, parts, centroids)
        blocks = lax.all_to_all(fresh, "items", 0, 0, axis_index_groups=ORDER)
        blocks = blocks.reshape(n_cents // TILE, 2, TILE, HALF).transpose(0, 2, 1, 3)
        current = blocks.reshape(n_cents, D)
    return current


def solution(mesh):
    in_specs = (P("items", None), P("items"), P("cents", None))
    out_specs = P("cents", None)
    return jax.shard_map(body, mesh=mesh, in_specs=in_specs, out_specs=out_specs, check_vma=False)
```

```python
import jax
import jax.numpy as jnp
from jax import lax
from jax.experimental import pallas as pl
from jax.experimental.pallas import tpu as pltpu
from jax.sharding import PartitionSpec as P

D = 1024
ITERS = 2
CHUNK = 128
PIECE = 384
EARLY = 2
LANES = 128
TILE = 8
HALF = D // 2
SUB = 4
prior_count = 2.0
X, Y = 4, 8
ORDER = [[x * Y + y for y in range(Y) for x in (0, 2, 1, 3)]]
Z, CORE = 8, 2
CENT_ORDER = [[z * CORE + core for core in range(CORE) for z in range(Z)]]
scale = D ** (-0.5)

f32, bf16 = jnp.float32, jnp.bfloat16
vmem = pl.BlockSpec(memory_space=pltpu.VMEM)
smem = pl.BlockSpec(memory_space=pltpu.SMEM)
hbm = pl.BlockSpec(memory_space=pltpu.HBM)


def norms_of(cents):
    wide = cents.astype(f32)
    return jnp.sum(wide * wide, axis=1, keepdims=True) * scale


def dot_chunk(cents, norms, rows_ref, start, size, score_ref):
    rows = rows_ref[pl.ds(start, size), :]
    dots = lax.dot_general(cents, rows, (((1,), (1,)), ((), ())), preferred_element_type=f32)
    score_ref[:, pl.ds(start, size)] = dots * (2.0 * scale) - norms


def logs_chunk(score_ref, start, size, logs_ref):
    score = score_ref[:, pl.ds(start, size)]
    top = jnp.max(score, axis=0, keepdims=True)
    logs = top + jnp.log(jnp.sum(jnp.exp(score - top), axis=0, keepdims=True))
    for peer in range(logs_ref.shape[0]):
        logs_ref[peer, :, pl.ds(start, size)] = logs


def score_span(cents, norms, rows_ref, first, last, score_ref, logs_ref):
    for start in range(first, last, CHUNK):
        dot_chunk(cents, norms, rows_ref, start, CHUNK, score_ref)
        logs_chunk(score_ref, start, CHUNK, logs_ref)


def first_scores(
    count_ref, place_ref, rows_hbm, cents_hbm, rows_ref, score_ref, logs_ref, known_ref, cents_ref, sems
):
    total = rows_ref.shape[0]
    starts = range(0, total, PIECE)
    cents_copy = pltpu.make_async_copy(cents_hbm, cents_ref, sems.at[len(starts)])
    cents_copy.start()
    copies = [
        pltpu.make_async_copy(
            rows_hbm.at[pl.ds(start, PIECE)], rows_ref.at[pl.ds(start, PIECE)], sems.at[i]
        )
        for i, start in enumerate(starts)
    ]
    for copy in copies:
        copy.start()
    known_ref[0] = count_ref[0]
    known_ref[1] = place_ref[0]
    cents_copy.wait()
    cents = cents_ref[...]
    norms = norms_of(cents)
    for copy in copies[:EARLY]:
        copy.wait()
    score_span(cents, norms, rows_ref, 0, EARLY * PIECE, score_ref, logs_ref)
    for copy in copies[EARLY:]:
        copy.wait()
    score_span(cents, norms, rows_ref, EARLY * PIECE, total, score_ref, logs_ref)


def later_scores(rows_ref, cents_ref, score_ref, logs_ref):
    cents = cents_ref[...]
    score_span(cents, norms_of(cents), rows_ref, 0, rows_ref.shape[0], score_ref, logs_ref)


def moments(known_ref, logs_ref, score_ref, rows_ref, out_ref):
    peers, _, total = logs_ref.shape
    n_cents = score_ref.shape[0]
    high = logs_ref[0]
    for peer in range(1, peers):
        high = jnp.maximum(high, logs_ref[peer])
    mass_all = jnp.exp(logs_ref[0] - high)
    for peer in range(1, peers):
        mass_all = mass_all + jnp.exp(logs_ref[peer] - high)
    logs = high + jnp.log(mass_all)
    valid = lax.broadcasted_iota(jnp.int32, (1, total), 1) < known_ref[0]
    resp = jnp.where(valid, jnp.exp(score_ref[...] - logs), 0.0).astype(bf16)
    mass = jnp.sum(resp.astype(f32), axis=1, keepdims=True)
    moment = jnp.dot(resp, rows_ref[...], preferred_element_type=f32)
    groups, halves = out_ref.shape[:2]
    pieces = HALF // LANES
    for half in range(halves):
        for piece in range(pieces):
            start = half * HALF + piece * LANES
            tile = moment[:, start : start + LANES].astype(bf16).reshape(groups, 2, SUB, LANES)
            for low in range(2):
                out_ref[:, half, low * pieces + piece] = tile[:, low]
    mass_high = mass.astype(bf16).astype(f32)
    lanes = lax.broadcasted_iota(jnp.int32, (n_cents, LANES), 1)
    masses = jnp.where(lanes % 2 == 0, mass_high, mass - mass_high).reshape(groups, 2, SUB, LANES)
    lanes = lax.broadcasted_iota(jnp.int32, (groups, SUB, LANES), 2)
    tile = jnp.where(lanes < 2, masses[:, 0], masses[:, 1]).astype(bf16)
    for half in range(halves):
        out_ref[:, half, 2 * pieces] = tile


def update(parts_ref, before, out_ref):
    sums = parts_ref[0].astype(f32)
    for part in range(1, parts_ref.shape[0]):
        sums = sums + parts_ref[part].astype(f32)
    pieces = HALF // LANES
    masses = sums[2 * pieces]
    rows = []
    for low in range(2):
        mass = masses[:, 2 * low : 2 * low + 1] + masses[:, 2 * low + 1 : 2 * low + 2]
        moment = jnp.concatenate([sums[low * pieces + piece] for piece in range(pieces)], axis=1)
        old = before[low * SUB : (low + 1) * SUB]
        rows.append((moment + prior_count * old) / (mass + prior_count))
    fresh = jnp.concatenate(rows, axis=0).astype(bf16)
    for part in range(out_ref.shape[0]):
        out_ref[part] = fresh


def first_update(known_ref, parts_ref, cents_ref, out_ref):
    place = known_ref[1]
    row = pl.multiple_of(place // 2 * TILE, TILE)
    near = cents_ref[pl.ds(row, TILE), :].astype(f32)
    update(parts_ref, jnp.where(place % 2 == 0, near[:, :HALF], near[:, HALF:]), out_ref)


def later_update(parts_ref, fresh_ref, out_ref):
    update(parts_ref, fresh_ref[0].astype(f32), out_ref)


def params(mib):
    return pltpu.CompilerParams(vmem_limit_bytes=mib << 20)


def body(embeddings, counts, centroids):
    total, n_cents = embeddings.shape[0], centroids.shape[0]
    n_items, n_split = lax.axis_size("items"), lax.axis_size("cents")
    item = lax.axis_index("items").astype(jnp.int32)
    x = item // Y
    place = (item % Y * X + x // 2 + x % 2 * 2)[None]
    score_shape = pltpu.VMEM((n_cents, total), f32)
    logs_shape = pltpu.VMEM((n_split, 1, total), f32)
    sent_shape = pltpu.VMEM((n_cents // TILE, 2, 2 * HALF // LANES + 1, SUB, LANES), bf16)
    block_shape = pltpu.VMEM((n_items, TILE, HALF), bf16)

    rows, score, logs, known = pl.pallas_call(
        first_scores,
        out_shape=(pltpu.VMEM(embeddings.shape, bf16), score_shape, logs_shape, pltpu.SMEM((2,), jnp.int32)),
        in_specs=[smem, smem, hbm, hbm],
        out_specs=(vmem, vmem, vmem, smem),
        scratch_shapes=[
            pltpu.VMEM(centroids.shape, bf16),
            pltpu.SemaphoreType.DMA((total // PIECE + 1,)),
        ],
        compiler_params=params(57),
        name="first_scores",
    )(counts, place, embeddings, centroids)
    fresh = current = None
    for step in range(ITERS):
        if step:
            score, logs = pl.pallas_call(
                later_scores,
                out_shape=(score_shape, logs_shape),
                in_specs=[vmem, vmem],
                out_specs=(vmem, vmem),
                compiler_params=params(16),
                name="later_scores",
            )(rows, current)
        logs = lax.all_to_all(logs, "cents", 0, 0, axis_index_groups=CENT_ORDER)
        sent = pl.pallas_call(
            moments,
            out_shape=sent_shape,
            in_specs=[smem, vmem, vmem, vmem],
            out_specs=vmem,
            compiler_params=params(16),
            name="moments",
        )(known, logs, score, rows)
        parts = lax.all_to_all(sent.reshape(n_items, *sent.shape[2:]), "items", 0, 0, axis_index_groups=ORDER)
        if step:
            fresh = pl.pallas_call(
                later_update,
                out_shape=block_shape,
                in_specs=[vmem, vmem],
                out_specs=vmem,
                compiler_params=params(16),
                name="later_update",
            )(parts, fresh)
        else:
            fresh = pl.pallas_call(
                first_update,
                out_shape=block_shape,
                in_specs=[smem, vmem, vmem],
                out_specs=vmem,
                compiler_params=params(16),
                name="first_update",
            )(known, parts, centroids)
        blocks = lax.all_to_all(fresh, "items", 0, 0, axis_index_groups=ORDER)
        blocks = blocks.reshape(n_cents // TILE, 2, TILE, HALF).transpose(0, 2, 1, 3)
        current = blocks.reshape(n_cents, D)
    return current


def solution(mesh):
    in_specs = (P("items", None), P("items"), P("cents", None))
    out_specs = P("cents", None)
    return jax.shard_map(body, mesh=mesh, in_specs=in_specs, out_specs=out_specs, check_vma=False)
```
